32 devices in a mesh: row: 8 (over z, core), col: 4 (over y, x).
Axes of the slice: x: 2, y: 2, z: 4, core: 2. Of those that a mesh axis runs over, the one named last changes fastest.
Arguments:
- base_weight: bfloat16 [16384, 49152], P('row', 'col'), may hold values from -6 to 6
- left_factor: float32 [16384, 256], P('row', 'col'), may hold values from -6 to 6
- right_factor: float32 [256, 49152], P('row', 'col'), may hold values from -0.375 to 0.375
Outputs:
- merged: bfloat16 [16384, 49152], P(None, ('row', 'col'))
The draws below stay inside these ranges and needn't reach their ends.
All inputs are finite; a program needn't handle non-finite values.
Results may differ from the reference program's by a relative error of at most 0.001.
Values may be sent and summed in bfloat16 or wider, within the bound.
A program may use at most 256 MiB of HBM per device.

```python
import jax
import jax.numpy as jnp
from jax import lax

D = 16384
FF = 49152
RANK = 256
N_ROW = 8


def steps_of(stream_key, shape, pieces, least, high):
    loudness = 1.0
    for dim, parts in pieces:
        draws = jax.random.uniform(jax.random.fold_in(jax.random.fold_in(stream_key, 6), dim), (parts,), jnp.float32, least / len(pieces), high / len(pieces))
        loudness = loudness * jnp.repeat(jnp.exp(draws), shape[dim] // parts).reshape((-1,) + (1,) * (len(shape) - 1 - dim))
    return loudness


def centred(key, shape, spread, most, split=(), dtype=jnp.bfloat16):
    result = jax.random.normal(key, shape, jnp.float32) * spread
    if len(split) > 0:
        result = steps_of(key, shape, split, -0.22, 0.18) * result
    return jnp.clip(result, min=-most, max=most).astype(dtype)


def setup_inputs(seed: int = 0) -> dict:
    key_list = jax.random.split(jax.random.key(seed), 4)
    base_weight = centred(key_list[0], (D, FF), 1.0, 6.0, ((0, 8), (1, 4)))
    left_factor = centred(key_list[1], (D, RANK), 1.0, 6.0, ((0, 8), (1, 4)), jnp.float32)
    right_factor = centred(key_list[2], (RANK, FF), RANK ** -0.5, 0.375, ((0, 8), (1, 4)), jnp.float32)
    return {"base_weight": base_weight, "left_factor": left_factor, "right_factor": right_factor}


def reference(base_weight, left_factor, right_factor):
    left_blocks = left_factor.reshape(N_ROW, D // N_ROW, RANK)
    base_blocks = base_weight.reshape(N_ROW, D // N_ROW, FF)

    def merge_block(pair):
        left_block, base_block = pair
        delta = jnp.dot(left_block, right_factor, precision=lax.Precision.HIGHEST, preferred_element_type=jnp.float32)
        return (base_block.astype(jnp.float32) + delta).astype(jnp.bfloat16)

    merged = lax.map(merge_block, (left_blocks, base_blocks))
    return merged.reshape(D, FF)
```

```python
import functools

import jax
import jax.numpy as jnp
from jax import lax
from jax.experimental import pallas as pl
from jax.experimental.pallas import tpu as pltpu
from jax.sharding import PartitionSpec as P

CHUNKS = 8
AHEAD = 2
MESH = pl.DeviceIdType.MESH


def transport(nr, nc, base, left, right, served, left_all, right_all, mid, mid_right, *sems):
    (a_send, a_recv, b_send, b_recv, ra_send, ra_recv, rb_send, rb_recv,
     l1_send, l1_recv, l2_send, l2_recv, l3_send, l3_recv, own_sem) = sems
    ng = nr // nc
    half = nr // 2
    height = base.shape[0]
    width = base.shape[1] // nr
    depth = right.shape[0]
    rank, left_width = left.shape
    step = height // CHUNKS
    r = lax.axis_index("row")
    c = lax.axis_index("col")
    sibling = r + 1 - 2 * lax.rem(r, 2)

    def remote(src, dst, send, recv, row, col):
        return pltpu.make_async_remote_copy(
            src_ref=src, dst_ref=dst, send_sem=send, recv_sem=recv, device_id=(row, col), device_id_type=MESH
        )

    def shifted(value, by, size):
        return lax.rem(value + by + size, size)

    def across(k, dj, g, src, final, middle, rows, send, recv, act):
        j = shifted(c, dj, nc)
        here = c * ng + g == r
        at = pl.ds(pl.multiple_of(k * rows, 8), rows)
        source = src.at[at, pl.ds(pl.multiple_of((g * nc + j) * width, 128), width)]
        sem = (k, dj - 1, g)

        @pl.when(here)
        def _():
            to = final.at[pl.ds(pl.multiple_of(r * src.shape[0] + k * rows, 8), rows), :]
            act(remote(source, to, send.at[sem], recv.at[sem], r, j))

        @pl.when(jnp.logical_not(here))
        def _():
            to = middle.at[c, g, at, :]
            act(remote(source, to, send.at[sem], recv.at[sem], r, j))

    def start(copy):
        copy.start()

    def wait_send(copy):
        copy.wait_send()

    def arrived(k, ds, g, src, final, middle, rows, send, recv):
        at = pl.ds(pl.multiple_of(k * rows, 8), rows)
        s = shifted(c, -ds, nc)
        here = s * ng + g == r
        sem = (k, ds - 1, g)

        @pl.when(here)
        def _():
            to = final.at[pl.ds(pl.multiple_of(r * src.shape[0] + k * rows, 8), rows), :]
            remote(to, to, send.at[sem], recv.at[sem], r, s).wait_recv()

        @pl.when(jnp.logical_not(here))
        def _():
            to = middle.at[s, g, at, :]
            remote(to, to, send.at[sem], recv.at[sem], r, s).wait_recv()

    def along(k, ds, g, src, final, middle, rows, send, recv, own, act, act_own):
        at = pl.ds(pl.multiple_of(k * rows, 8), rows)
        s = shifted(c, -ds, nc)
        to_row = s * ng + g
        if ds == 0:
            source = src.at[at, pl.ds(pl.multiple_of((g * nc + c) * width, 128), width)]
        else:
            source = middle.at[s, g, at, :]
        to = final.at[pl.ds(pl.multiple_of(r * src.shape[0] + k * rows, 8), rows), :]

        @pl.when(to_row != r)
        def _():
            act(remote(source, to, send.at[k, ds, g], recv.at[k, r], to_row, c))

        if ds == 0:
            @pl.when(to_row == r)
            def _():
                act_own(pltpu.make_async_copy(source, to, own.at[k]))

    def received(k, dq, final, rows, total, send, recv):
        q = shifted(r, -dq, nr)
        to = final.at[pl.ds(pl.multiple_of(q * total + k * rows, 8), rows), :]
        remote(to, to, send.at[k, 0, 0], recv.at[k, q], q, c).wait_recv()

    big = (base, served, mid, step)
    small = (right, right_all, mid_right, depth)
    own_big = own_sem.at[pl.ds(0, CHUNKS)]
    own_small = own_sem.at[pl.ds(CHUNKS, 1)]

    def each_across(k, arrays, send, recv, act):
        for g in range(ng):
            for dj in range(1, nc):
                across(k, dj, g, *arrays, send, recv, act)

    def each_along(k, shifts, arrays, send, recv, own, act, act_own):
        for ds in shifts:
            for g in range(ng):
                along(k, ds, g, *arrays, send, recv, own, act, act_own)

    def block(s, q):
        return left_all.at[
            pl.ds(pl.multiple_of(s * rank, 8), rank), pl.ds(pl.multiple_of(q * left_width, 128), left_width)
        ]

    def first_left(d):
        return remote(left, block(c, r), l1_send.at[d - 1], l1_recv.at[d - 1], shifted(r, 2 * d, nr), c)

    def second_left(d, dj):
        q = shifted(r, -2 * d, nr)
        source = left if d == 0 else block(c, q)
        return remote(source, block(c, q), l2_send.at[d, dj - 1], l2_recv.at[d, dj - 1], r, shifted(c, dj, nc))

    def third_left(d, ds):
        q = shifted(r, -2 * d, nr)
        s = shifted(c, -ds, nc)
        source = left if d == 0 and ds == 0 else block(s, q)
        return remote(source, block(s, q), l3_send.at[d, ds], l3_recv.at[d, ds], sibling, c)

    def got(sems_send, sems_recv, s, q):
        remote(block(s, q), block(s, q), sems_send, sems_recv, r, shifted(c, 1, nc)).wait_recv()

    barrier = pltpu.get_barrier_semaphore()
    for dj in range(1, nc):
        pl.semaphore_signal(barrier, inc=1, device_id=(r, shifted(c, dj, nc)), device_id_type=MESH)
    for dq in range(1, nr):
        pl.semaphore_signal(barrier, inc=1, device_id=(shifted(r, dq, nr), c), device_id_type=MESH)
    pl.semaphore_wait(barrier, nc + nr - 2)

    def open_chunk(k):
        each_across(k, big, a_send, a_recv, start)
        each_along(k, (0,), big, b_send, b_recv, own_big, start, start)

    each_across(0, big, a_send, a_recv, start)
    for d in range(1, half):
        first_left(d).start()
    each_along(0, (0,), big, b_send, b_recv, own_big, start, start)
    each_across(0, small, ra_send, ra_recv, start)
    each_along(0, (0,), small, rb_send, rb_recv, own_small, start, start)
    own_left = pltpu.make_async_copy(left, block(c, r), own_sem.at[CHUNKS + 1])
    own_left.start()

    @pl.loop(1, AHEAD)
    def _(k):
        open_chunk(k)

    def forward(k):
        for g in range(ng):
            for ds in range(1, nc):
                arrived(k, ds, g, *big, a_send, a_recv)
        each_along(k, range(1, nc), big, b_send, b_recv, own_big, start, start)

    @pl.loop(0, CHUNKS)
    def _(k):
        @pl.when(k + AHEAD < CHUNKS)
        def _():
            open_chunk(k + AHEAD)

        forward(k)

        @pl.when(k == 0)
        def _():
            for g in range(ng):
                for ds in range(1, nc):
                    arrived(0, ds, g, *small, ra_send, ra_recv)
            each_along(0, range(1, nc), small, rb_send, rb_recv, own_small, start, start)

    for d in range(half):
        if d > 0:
            got(l1_send.at[d - 1], l1_recv.at[d - 1], c, shifted(r, -2 * d, nr))
        for dj in range(1, nc):
            second_left(d, dj).start()
        third_left(d, 0).start()
    for d in range(half):
        for ds in range(1, nc):
            got(l2_send.at[d, ds - 1], l2_recv.at[d, ds - 1], shifted(c, -ds, nc), shifted(r, -2 * d, nr))
            third_left(d, ds).start()
    for d in range(half):
        for ds in range(nc):
            got(l3_send.at[d, ds], l3_recv.at[d, ds], shifted(c, -ds, nc), shifted(sibling, -2 * d, nr))
            third_left(d, ds).wait_send()
        for dj in range(1, nc):
            second_left(d, dj).wait_send()
        if d > 0:
            first_left(d).wait_send()
    own_left.wait()

    def finish(copy):
        copy.wait()

    def drain(k, arrays, a, b_s, b_r, own):
        each_across(k, arrays, *a, wait_send)
        each_along(k, range(nc), arrays, b_s, b_r, own, wait_send, finish)
        for dq in range(1, nr):
            received(k, dq, arrays[1], arrays[3], arrays[0].shape[0], b_s, b_r)

    drain(0, small, (ra_send, ra_recv), rb_send, rb_recv, own_small)

    @pl.loop(0, CHUNKS)
    def _(k):
        drain(k, big, (a_send, a_recv), b_send, b_recv, own_big)


def move(base_weight, left_turned, right_factor):
    nr = lax.axis_size("row")
    nc = lax.axis_size("col")
    ng = nr // nc
    half = nr // 2
    height, stored_width = base_weight.shape
    width = stored_width // nr
    depth = right_factor.shape[0]
    rank, left_width = left_turned.shape
    out = jax.ShapeDtypeStruct
    dma = pltpu.SemaphoreType.DMA
    anywhere = pl.BlockSpec(memory_space=pl.ANY)

    def stage_sems(chunks):
        a = (chunks, nc - 1, ng)
        return [dma(a), dma(a), dma((chunks, nc, ng)), dma((chunks, nr))]

    return pl.pallas_call(
        functools.partial(transport, nr, nc),
        out_shape=[
            out((nr * height, width), base_weight.dtype),
            out((nc * rank, nr * left_width), left_turned.dtype),
            out((nr * depth, width), right_factor.dtype),
            out((nc, ng, height, width), base_weight.dtype),
            out((nc, ng, depth, width), right_factor.dtype),
        ],
        in_specs=[anywhere] * 3,
        out_specs=[anywhere] * 5,
        scratch_shapes=[
            *stage_sems(CHUNKS),
            *stage_sems(1),
            dma((half - 1,)), dma((half - 1,)),
            dma((half, nc - 1)), dma((half, nc - 1)),
            dma((half, nc)), dma((half, nc)),
            dma((CHUNKS + 2,)),
        ],
        compiler_params=pltpu.CompilerParams(collective_id=0, has_side_effects=True),
    )(base_weight, left_turned, right_factor)


def body(base_weight, left_factor, right_factor):
    served, left_all, right_all, _, _ = move(base_weight, left_factor.T, right_factor)
    delta = lax.dot_general(
        left_all, right_all, (((0,), (0,)), ((), ())),
        precision=lax.Precision.HIGH, preferred_element_type=jnp.float32,
    )
    return (served.astype(jnp.float32) + delta).astype(jnp.bfloat16)


def solution(mesh):
    placed = (P("row", "col"), P("row", "col"), P("row", "col"))
    return jax.shard_map(
        body, mesh=mesh, in_specs=placed, out_specs=P(None, ("row", "col")), check_vma=False
    )
```

```python
import functools

import jax
import jax.numpy as jnp
from jax import lax
from jax.experimental import pallas as pl
from jax.experimental.pallas import tpu as pltpu
from jax.sharding import PartitionSpec as P

CHUNKS = 8
AHEAD = 2
DELAY = 6
MESH = pl.DeviceIdType.MESH


def transport(nr, nc, base, left, right, served, left_all, right_all, mid, mid_right, *sems):
    (a_send, a_recv, b_send, b_recv, ra_send, ra_recv, rb_send, rb_recv,
     l1_send, l1_recv, l2_send, l2_recv, l3_send, l3_recv, own_sem) = sems
    ng = nr // nc
    half = nr // 2
    height = base.shape[0]
    width = base.shape[1] // nr
    depth = right.shape[0]
    rank, left_width = left.shape
    step = height // CHUNKS
    r = lax.axis_index("row")
    c = lax.axis_index("col")
    sibling = r + 1 - 2 * lax.rem(r, 2)

    def remote(src, dst, send, recv, row, col):
        return pltpu.make_async_remote_copy(
            src_ref=src, dst_ref=dst, send_sem=send, recv_sem=recv, device_id=(row, col), device_id_type=MESH
        )

    def shifted(value, by, size):
        return lax.rem(value + by + size, size)

    def across(k, dj, g, src, final, middle, rows, send, recv, act):
        j = shifted(c, dj, nc)
        here = c * ng + g == r
        at = pl.ds(pl.multiple_of(k * rows, 8), rows)
        source = src.at[at, pl.ds(pl.multiple_of((g * nc + j) * width, 128), width)]
        sem = (k, dj - 1, g)

        @pl.when(here)
        def _():
            to = final.at[pl.ds(pl.multiple_of(r * src.shape[0] + k * rows, 8), rows), :]
            act(remote(source, to, send.at[sem], recv.at[sem], r, j))

        @pl.when(jnp.logical_not(here))
        def _():
            to = middle.at[c, g, at, :]
            act(remote(source, to, send.at[sem], recv.at[sem], r, j))

    def start(copy):
        copy.start()

    def wait_send(copy):
        copy.wait_send()

    def arrived(k, ds, g, src, final, middle, rows, send, recv):
        at = pl.ds(pl.multiple_of(k * rows, 8), rows)
        s = shifted(c, -ds, nc)
        here = s * ng + g == r
        sem = (k, ds - 1, g)

        @pl.when(here)
        def _():
            to = final.at[pl.ds(pl.multiple_of(r * src.shape[0] + k * rows, 8), rows), :]
            remote(to, to, send.at[sem], recv.at[sem], r, s).wait_recv()

        @pl.when(jnp.logical_not(here))
        def _():
            to = middle.at[s, g, at, :]
            remote(to, to, send.at[sem], recv.at[sem], r, s).wait_recv()

    def along(k, ds, g, src, final, middle, rows, send, recv, own, act, act_own):
        at = pl.ds(pl.multiple_of(k * rows, 8), rows)
        s = shifted(c, -ds, nc)
        to_row = s * ng + g
        if ds == 0:
            source = src.at[at, pl.ds(pl.multiple_of((g * nc + c) * width, 128), width)]
        else:
            source = middle.at[s, g, at, :]
        to = final.at[pl.ds(pl.multiple_of(r * src.shape[0] + k * rows, 8), rows), :]

        @pl.when(to_row != r)
        def _():
            act(remote(source, to, send.at[k, ds, g], recv.at[k, r], to_row, c))

        if ds == 0:
            @pl.when(to_row == r)
            def _():
                act_own(pltpu.make_async_copy(source, to, own.at[k]))

    def received(k, dq, final, rows, total, send, recv):
        q = shifted(r, -dq, nr)
        to = final.at[pl.ds(pl.multiple_of(q * total + k * rows, 8), rows), :]
        remote(to, to, send.at[k, 0, 0], recv.at[k, q], q, c).wait_recv()

    big = (base, served, mid, step)
    small = (right, right_all, mid_right, depth)
    own_big = own_sem.at[pl.ds(0, CHUNKS)]
    own_small = own_sem.at[pl.ds(CHUNKS, 1)]

    def each_across(k, arrays, send, recv, act):
        for dj in range(1, nc):
            for g in range(ng):
                across(k, dj, g, *arrays, send, recv, act)

    def each_along(k, shifts, arrays, send, recv, own, act, act_own):
        for ds in shifts:
            for g in range(ng):
                along(k, ds, g, *arrays, send, recv, own, act, act_own)

    def block(s, q):
        return left_all.at[
            pl.ds(pl.multiple_of(s * rank, 8), rank), pl.ds(pl.multiple_of(q * left_width, 128), left_width)
        ]

    def first_left(d):
        return remote(left, block(c, r), l1_send.at[d - 1], l1_recv.at[d - 1], shifted(r, 2 * d, nr), c)

    def second_left(d, dj):
        q = shifted(r, -2 * d, nr)
        source = left if d == 0 else block(c, q)
        return remote(source, block(c, q), l2_send.at[d, dj - 1], l2_recv.at[d, dj - 1], r, shifted(c, dj, nc))

    def third_left(d, ds):
        q = shifted(r, -2 * d, nr)
        s = shifted(c, -ds, nc)
        source = left if d == 0 and ds == 0 else block(s, q)
        return remote(source, block(s, q), l3_send.at[d, ds], l3_recv.at[d, ds], sibling, c)

    def got(sems_send, sems_recv, s, q):
        remote(block(s, q), block(s, q), sems_send, sems_recv, r, shifted(c, 1, nc)).wait_recv()

    barrier = pltpu.get_barrier_semaphore()
    for dj in range(1, nc):
        pl.semaphore_signal(barrier, inc=1, device_id=(r, shifted(c, dj, nc)), device_id_type=MESH)
    for dq in range(1, nr):
        pl.semaphore_signal(barrier, inc=1, device_id=(shifted(r, dq, nr), c), device_id_type=MESH)
    pl.semaphore_wait(barrier, nc + nr - 2)

    each_across(0, big, a_send, a_recv, start)
    for d in range(1, half):
        first_left(d).start()
    each_across(0, small, ra_send, ra_recv, start)
    each_along(0, (0,), small, rb_send, rb_recv, own_small, start, start)
    own_left = pltpu.make_async_copy(left, block(c, r), own_sem.at[CHUNKS + 1])
    own_left.start()

    @pl.loop(1, AHEAD)
    def _(k):
        each_across(k, big, a_send, a_recv, start)

    plane = r // ng
    at_end = jnp.logical_or(r < ng, r >= nr - ng)

    def forward(k):
        for ds in range(nc):
            s = shifted(c, -ds, nc)
            late = jnp.logical_and(at_end, jnp.abs(s - plane) >= 2)
            turn = jnp.where(late, k - DELAY, k)

            @pl.when(jnp.logical_and(turn >= 0, turn < CHUNKS))
            def _():
                for g in range(ng):
                    if ds > 0:
                        arrived(turn, ds, g, *big, a_send, a_recv)
                    along(turn, ds, g, *big, b_send, b_recv, own_big, start, start)

    @pl.loop(0, CHUNKS + DELAY)
    def _(k):
        @pl.when(k + AHEAD < CHUNKS)
        def _():
            each_across(k + AHEAD, big, a_send, a_recv, start)

        forward(k)

        @pl.when(k == 0)
        def _():
            for g in range(ng):
                for ds in range(1, nc):
                    arrived(0, ds, g, *small, ra_send, ra_recv)
            each_along(0, range(1, nc), small, rb_send, rb_recv, own_small, start, start)

    for d in range(half):
        if d > 0:
            got(l1_send.at[d - 1], l1_recv.at[d - 1], c, shifted(r, -2 * d, nr))
        for dj in range(1, nc):
            second_left(d, dj).start()
        third_left(d, 0).start()
    for d in range(half):
        for ds in range(1, nc):
            got(l2_send.at[d, ds - 1], l2_recv.at[d, ds - 1], shifted(c, -ds, nc), shifted(r, -2 * d, nr))
            third_left(d, ds).start()
    for d in range(half):
        for ds in range(nc):
            got(l3_send.at[d, ds], l3_recv.at[d, ds], shifted(c, -ds, nc), shifted(sibling, -2 * d, nr))
            third_left(d, ds).wait_send()
        for dj in range(1, nc):
            second_left(d, dj).wait_send()
        if d > 0:
            first_left(d).wait_send()
    own_left.wait()

    def finish(copy):
        copy.wait()

    def drain(k, arrays, a, b_s, b_r, own):
        each_across(k, arrays, *a, wait_send)
        each_along(k, range(nc), arrays, b_s, b_r, own, wait_send, finish)
        for dq in range(1, nr):
            received(k, dq, arrays[1], arrays[3], arrays[0].shape[0], b_s, b_r)

    drain(0, small, (ra_send, ra_recv), rb_send, rb_recv, own_small)

    @pl.loop(0, CHUNKS)
    def _(k):
        drain(k, big, (a_send, a_recv), b_send, b_recv, own_big)


def move(base_weight, left_turned, right_factor):
    nr = lax.axis_size("row")
    nc = lax.axis_size("col")
    ng = nr // nc
    half = nr // 2
    height, stored_width = base_weight.shape
    width = stored_width // nr
    depth = right_factor.shape[0]
    rank, left_width = left_turned.shape
    out = jax.ShapeDtypeStruct
    dma = pltpu.SemaphoreType.DMA
    anywhere = pl.BlockSpec(memory_space=pl.ANY)

    def stage_sems(chunks):
        a = (chunks, nc - 1, ng)
        return [dma(a), dma(a), dma((chunks, nc, ng)), dma((chunks, nr))]

    return pl.pallas_call(
        functools.partial(transport, nr, nc),
        out_shape=[
            out((nr * height, width), base_weight.dtype),
            out((nc * rank, nr * left_width), left_turned.dtype),
            out((nr * depth, width), right_factor.dtype),
            out((nc, ng, height, width), base_weight.dtype),
            out((nc, ng, depth, width), right_factor.dtype),
        ],
        in_specs=[anywhere] * 3,
        out_specs=[anywhere] * 5,
        scratch_shapes=[
            *stage_sems(CHUNKS),
            *stage_sems(1),
            dma((half - 1,)), dma((half - 1,)),
            dma((half, nc - 1)), dma((half, nc - 1)),
            dma((half, nc)), dma((half, nc)),
            dma((CHUNKS + 2,)),
        ],
        compiler_params=pltpu.CompilerParams(collective_id=0, has_side_effects=True),
    )(base_weight, left_turned, right_factor)


def body(base_weight, left_factor, right_factor):
    served, left_all, right_all, _, _ = move(base_weight, left_factor.T, right_factor)
    delta = lax.dot_general(
        left_all, right_all, (((0,), (0,)), ((), ())),
        precision=lax.Precision.HIGH, preferred_element_type=jnp.float32,
    )
    return (served.astype(jnp.float32) + delta).astype(jnp.bfloat16)


def solution(mesh):
    placed = (P("row", "col"), P("row", "col"), P("row", "col"))
    return jax.shard_map(
        body, mesh=mesh, in_specs=placed, out_specs=P(None, ("row", "col")), check_vma=False
    )
```
